32 devices in a mesh: dp: 16 (over z, x, core), frame: 2 (over y).
Axes of the slice: x: 2, y: 2, z: 4, core: 2. Of those that a mesh axis runs over, the one named last changes fastest.
Arguments:
- video_tokens: bfloat16 [256, 2, 32, 1024], P('dp', 'frame'), may hold values from -14 to 14
- pool_weight: bfloat16 [2, 16, 32], P('frame'), may hold values from -1 to 1
- text_states: bfloat16 [256, 77, 1600], P(('dp', 'frame')), may hold values from -6 to 6
- norm_gain: float32 [1600], replicated, may hold values from 0.5 to 1.5
- lengths: int32 [256], P(('dp', 'frame')), may hold values from 1 to 77
- cotangent: bfloat16 [256, 77, 1600], P(('dp', 'frame')), may hold values from -6 to 6
- query_weight: bfloat16 [1600, 896], P('dp'), may hold values from -0.15625 to 0.15625
- key_weight: bfloat16 [1024, 896], P('dp'), may hold values from -0.1875 to 0.1875
- value_weight: bfloat16 [1024, 896], P('dp'), may hold values from -0.1875 to 0.1875
- out_weight: bfloat16 [896, 1600], P('dp'), may hold values from -0.1875 to 0.1875
Outputs:
- grad_text: bfloat16 [256, 77, 1600], P(('dp', 'frame'))
- grad_pooled: bfloat16 [256, 32, 1024], P('dp', 'frame')
The draws below stay inside these ranges and needn't reach their ends.
Inputs may be any that keep to these rules, and one draw needn't show every extreme that they name: `lengths`: text positions at or after a clip's length are padding.
All inputs are finite; a program needn't handle non-finite values.
Results may differ from the reference program's by a relative error of at most 0.02.
The reference program's roundings to bfloat16 on the way count: a program that leaves them out, or rounds other values in their place, can miss the bound.
Values may be sent and summed in bfloat16 or wider, within the bound.
No kernel may reach another device: no remote copies, remote signals or barrier semaphores. Data moves between devices by JAX's collectives and lax.ppermute only.
A program may use at most 64 MiB of HBM per device.

```python
import jax
import jax.numpy as jnp
from jax import lax

D = 1600
V = 1024
HEADS = 14
HD = 64
TEXT = 77
PATCH = 32
LAT_F = 16
CLIP_DEV = 16
HW = 896
FRAMES = 2
LATENTS = 32
CLIPS = 256


def draw_video_tokens(key, part):
    array_shape = (CLIPS, FRAMES, PATCH, V)
    result = jnp.clip(jax.random.normal(key, array_shape, jnp.float32), -6.0, 6.0)
    return result.astype(jnp.bfloat16)


def place_ends(values, stream_key, low, high):
    extent = values.shape
    spot = [jax.random.randint(jax.random.fold_in(stream_key, axis), (), 0, extent[axis]) for axis in range(len(extent))]
    values = values.at[tuple(spot)].set(low)
    longest = extent.index(max(extent))
    spot[longest] = (spot[longest] + 1) % extent[longest]
    return values.at[tuple(spot)].set(high)


def levels(key, shape, cuts, least, high):
    level = 1.0
    for dim, shards_of in cuts:
        draws = jax.random.uniform(jax.random.fold_in(jax.random.fold_in(key, 6), dim), (shards_of,), jnp.float32, least / len(cuts), high / len(cuts))
        level = level * jnp.repeat(jnp.exp(draws), shape[dim] // shards_of).reshape((-1,) + (1,) * (len(shape) - 1 - dim))
    return level


def centred(rng, shape, scale, most, shards=(), held_as=jnp.bfloat16):
    loudness = levels(rng, shape, shards, -0.22, 0.18) if shards else 1.0
    values = jax.random.normal(rng, shape, jnp.float32) * scale * loudness
    return jnp.minimum(jnp.maximum(values, -most), most).astype(held_as)


def setup_inputs(seed: int = 0) -> dict:
    splits = jax.random.split(jax.random.key(seed), 11)
    return {
        "video_tokens": draw_video_tokens(jax.random.fold_in(splits[10], 71), 0),
        "pool_weight": centred(splits[1], (FRAMES, LAT_F, PATCH), PATCH ** -0.5, 1.0, ((0, 2),)),
        "text_states": centred(splits[2], (CLIPS, TEXT, D), 1.0, 6.0, ((0, 32),)),
        "norm_gain": jnp.clip(1.0 + 0.1 * jax.random.normal(splits[3], (D,), jnp.float32), 0.5, 1.5),
        "lengths": place_ends(jax.random.randint(splits[4], (CLIPS,), 1, TEXT + 1), jax.random.fold_in(splits[4], 1), 1, TEXT).astype(jnp.int32),
        "cotangent": centred(splits[5], (CLIPS, TEXT, D), 1.0, 6.0, ((0, 32),)),
        "query_weight": centred(splits[6], (D, HW), D ** -0.5, 0.15625, ((0, 16),)),
        "key_weight": centred(splits[7], (V, HW), V ** -0.5, 0.1875, ((0, 16),)),
        "value_weight": centred(splits[8], (V, HW), V ** -0.5, 0.1875, ((0, 16),)),
        "out_weight": centred(splits[9], (HW, D), HW ** -0.5, 0.1875, ((0, 16),)),
    }


EPSILON = 1e-05

def product(left, right):
    return jnp.dot(left, right, preferred_element_type=jnp.float32)

def product_back(left, right):
    return lax.dot_general(left, right, (((1,), (1,)), ((), ())), preferred_element_type=jnp.float32)

def rounded(array):
    return lax.optimization_barrier(array.astype(jnp.bfloat16))

def split_heads(array, clip_count):
    return array.reshape(clip_count, -1, HEADS, HD).astype(jnp.float32)

def one_block(video_tokens, pool_weight, text_states, norm_gain, lengths, cotangent, query_weight, key_weight, value_weight, out_weight):
    clip_count = video_tokens.shape[0]
    highest = lax.Precision.HIGHEST
    score_scale = HD ** (-0.5)
    pooled = jnp.einsum('flp,cfpv->cflv', pool_weight.astype(jnp.float32), video_tokens.astype(jnp.float32), precision=highest)
    pooled = rounded(pooled).reshape(clip_count * LATENTS, V)
    key_rows = rounded(product(pooled, key_weight))
    value_rows = rounded(product(pooled, value_weight))
    text_rows = text_states.reshape(clip_count * TEXT, D).astype(jnp.float32)
    average = lax.optimization_barrier(jnp.mean(text_rows, axis=1, keepdims=True))
    centered = text_rows - average
    inverse = lax.rsqrt(lax.optimization_barrier(jnp.mean(centered * centered, axis=1, keepdims=True)) + EPSILON)
    unit_rows = centered * inverse
    normed = rounded(unit_rows * norm_gain)
    queries = rounded(product(normed, query_weight))
    query_heads = split_heads(queries, clip_count)
    key_heads = split_heads(key_rows, clip_count)
    value_heads = split_heads(value_rows, clip_count)
    scores = jnp.einsum('cthd,clhd->chtl', query_heads, key_heads, precision=highest) * score_scale
    row_max = lax.optimization_barrier(jnp.max(scores, axis=3, keepdims=True))
    shifted = jnp.exp(scores - row_max)
    attn_probs = shifted / lax.optimization_barrier(jnp.sum(shifted, axis=3, keepdims=True))
    probs_low = rounded(attn_probs).astype(jnp.float32)
    attended = rounded(jnp.einsum('chtl,clhd->cthd', probs_low, value_heads, precision=highest)).astype(jnp.float32)
    positions = jnp.arange(TEXT, dtype=jnp.int32)
    valid_mask = positions[None, :] < lengths[:, None]
    grad_out = jnp.where(valid_mask[:, :, None], cotangent, jnp.zeros_like(cotangent)).reshape(clip_count * TEXT, D)
    grad_att = rounded(product_back(grad_out, out_weight))
    grad_heads = split_heads(grad_att, clip_count)
    grad_probs = jnp.einsum('cthd,clhd->chtl', grad_heads, value_heads, precision=highest)
    row_term = jnp.einsum('cthd,cthd->cht', grad_heads, attended, precision=highest)[..., None]
    grad_scores = rounded(attn_probs * (grad_probs - row_term) * score_scale).astype(jnp.float32)
    grad_queries = rounded(jnp.einsum('chtl,clhd->cthd', grad_scores, key_heads, precision=highest)).reshape(clip_count * TEXT, HW)
    grad_keys = rounded(jnp.einsum('chtl,cthd->clhd', grad_scores, query_heads, precision=highest)).reshape(clip_count * LATENTS, HW)
    grad_values = rounded(jnp.einsum('chtl,cthd->clhd', probs_low, grad_heads, precision=highest)).reshape(clip_count * LATENTS, HW)
    grad_pooled = (product_back(grad_keys, key_weight) + product_back(grad_values, value_weight)).astype(jnp.bfloat16)
    grad_normed = product_back(grad_queries, query_weight)
    scaled_grad = grad_normed * norm_gain
    grad_rows = inverse * (scaled_grad - lax.optimization_barrier(jnp.mean(scaled_grad, axis=1, keepdims=True)) - unit_rows * lax.optimization_barrier(jnp.mean(scaled_grad * unit_rows, axis=1, keepdims=True)))
    return (grad_rows.astype(jnp.bfloat16).reshape(clip_count, TEXT, D), grad_pooled.reshape(clip_count, LATENTS, V))

def reference(video_tokens, pool_weight, text_states, norm_gain, lengths, cotangent, query_weight, key_weight, value_weight, out_weight):
    blocks = CLIPS // CLIP_DEV

    def process(pieces):
        return one_block(pieces[0], pool_weight, pieces[1], norm_gain, pieces[2], pieces[3], query_weight, key_weight, value_weight, out_weight)
    shaped = (video_tokens.reshape(blocks, CLIP_DEV, FRAMES, PATCH, V), text_states.reshape(blocks, CLIP_DEV, TEXT, D), lengths.reshape(blocks, CLIP_DEV), cotangent.reshape(blocks, CLIP_DEV, TEXT, D))
    grad_text, grad_pooled = lax.map(process, shaped)
    return (grad_text.reshape(CLIPS, TEXT, D), grad_pooled.reshape(CLIPS, LATENTS, V))
```

```python
import functools

import jax
import jax.numpy as jnp
from jax import lax
from jax.experimental import pallas as pl
from jax.experimental.pallas import tpu as pltpu
from jax.sharding import PartitionSpec as P


HD = 64
EPSILON = 1e-05
F32 = jnp.float32
BF16 = jnp.bfloat16
LANES = 128
NT = (((1,), (1,)), ((), ()))
TN = (((0,), (0,)), ((), ()))
VMEM = pl.BlockSpec(memory_space=pltpu.VMEM)
SMEM = pl.BlockSpec(memory_space=pltpu.SMEM)


def up(value, unit):
    return -(-value // unit) * unit


def spans(total, step):
    return [(i, min(step, total - i)) for i in range(0, total, step)]


def params():
    return pltpu.CompilerParams(vmem_limit_bytes=32 * 1024 * 1024)


def cost(flops, nbytes):
    return pl.CostEstimate(flops=flops, bytes_accessed=nbytes, transcendentals=0)


def relayed(count):
    return count // 4 == 4


def pieces_of(own, count):
    def move(array, pairs):
        return lax.ppermute(array, "dp", pairs)

    def along(pairs):
        return [(4 * a + i, 4 * b + i) for a, b in pairs for i in range(4)]

    def flip(mask):
        return [(i, i ^ mask) for i in range(count)]

    pieces = {0: own}
    if relayed(count):
        place = lax.axis_index("dp") // 4
        inner = (place == 1) | (place == 2)
        swap, ends = along([(1, 2), (2, 1)]), along([(1, 0), (2, 3)])
        pieces[4] = move(own, flip(4))
        first = move(own, swap)
        second = move(pieces[4], swap)
        pieces[8] = jnp.where(inner, first, move(first, ends))
        pieces[12] = jnp.where(inner, second, move(second, ends))
    else:
        for mask in range(4, count, 4):
            pieces[mask] = move(own, flip(mask))
    for mask in range(0, count, 4):
        if mask + 2 < count:
            pieces[mask + 2] = move(pieces[mask], flip(2))
    for mask in range(0, count, 2):
        pieces[mask + 1] = move(pieces[mask], flip(1))
    return [pieces[mask] for mask in range(count)]


def sources(count):
    me = lax.axis_index("dp")
    inner = lax.rem(lax.div(lax.div(me, 4) + 1, 2), 2)
    turn = 4 * inner if relayed(count) else 0
    return [me ^ m ^ turn if m >= 8 else me ^ m for m in range(count)]


def project_kernel(count, out_rows, *refs):
    pieces = refs[:count]
    pool_ref, cot_ref, kv_ref, wkv, gs_ref, loose, wo = refs[count:]
    rows, model = cot_ref.shape
    tiles, full, _ = gs_ref.shape
    width = tiles * LANES
    depth = wkv.shape[0] // count
    _, tall, wide = loose.shape
    if full > rows:
        for j in range(tiles):
            gs_ref[j, rows:full, :] = jnp.zeros((full - rows, LANES), F32)
    for piece, source in zip(pieces, sources(count)):
        wkv[pl.ds(pl.multiple_of(source * depth, depth), depth), :] = piece[0:depth, :]
        loose[source] = piece[depth : depth + tall, 0:wide]
    for p in range(count):
        wo[p * out_rows : (p + 1) * out_rows, :] = loose[p, 0:out_rows, :]
    for at, size in spans(2 * width, 256):
        made = jnp.dot(pool_ref[...], wkv[:, at : at + size], preferred_element_type=F32)
        if at + size <= width:
            made = made.astype(BF16) * HD ** (-0.5)
        elif at < width:
            lane = at + lax.broadcasted_iota(jnp.int32, made.shape, 1)
            made = made * jnp.where(lane < width, HD ** (-0.5), 1.0)
        kv_ref[:, at : at + size] = made.astype(BF16)
    for at, size in spans(width, 256):
        made = lax.dot_general(
            cot_ref[...], wo[at : at + size, :model], NT, preferred_element_type=F32
        )
        made = made.astype(BF16).astype(F32)
        for part in range(0, size, LANES):
            gs_ref[(at + part) // LANES, 0:rows, :] = made[:, part : part + LANES]


def norm_kernel(text_ref, gain_ref, normed_ref, mean_ref, inv_ref):
    rows = text_ref.shape[0]
    step = 88 if rows % 88 == 0 else rows

    for at, size in spans(rows, step):
        x = text_ref[at : at + size, :].astype(F32)
        mean = jnp.mean(x, axis=1, keepdims=True)
        centered = x - mean
        inverse = lax.rsqrt(jnp.mean(centered * centered, axis=1, keepdims=True) + EPSILON)
        normed_ref[at : at + size, :] = (centered * inverse * gain_ref[...]).astype(BF16)
        mean_ref[at : at + size, :] = jnp.broadcast_to(mean, (size, LANES))
        inv_ref[at : at + size, :] = jnp.broadcast_to(inverse, (size, LANES))


def attend_kernel(count, clips, frames, *refs):
    pieces = refs[:count]
    lengths_ref, normed_ref, gs_ref, kv_ref, wkv, gq_ref, pool_ref, wq = refs[
        count : count + 8
    ]
    slots, qs, gkv = refs[count + 8 :]
    depth = pieces[0].shape[0]
    width = kv_ref.shape[1] // 2
    rows = normed_ref.shape[0]
    tiles, full, _ = qs.shape
    times = full // clips
    lat = kv_ref.shape[0] // (frames * clips)
    latents = lat * frames
    scale = HD ** (-0.5)
    for piece, source in zip(pieces, sources(count)):
        slots[source] = piece[...]
    if full > rows:
        for j in range(tiles):
            qs[j, rows:full, :] = jnp.zeros((full - rows, LANES), F32)
    for p in range(count):
        wq[p * depth : (p + 1) * depth, :] = slots[p]
    for at, size in spans(width, 256):
        made = jnp.dot(normed_ref[...], wq[:, at : at + size], preferred_element_type=F32)
        made = made.astype(BF16).astype(F32)
        for part in range(0, size, LANES):
            qs[(at + part) // LANES, 0:rows, :] = made[:, part : part + LANES]

    def clip(c, carry):
        length = lengths_ref[c]
        valid = lax.broadcasted_iota(jnp.int32, (times, LANES), 0) < length
        starts = [
            pl.multiple_of((f * clips + c) * lat, lat) for f in range(frames)
        ]
        for first in range(0, tiles, 2):
            group = range(first, min(first + 2, tiles))
            at = first * LANES
            wide = len(group) * LANES
            heads = wide // HD
            q = jnp.concatenate(
                [qs[j, pl.ds(c, times, stride=clips), :].astype(BF16) for j in group], 1
            )
            g = jnp.concatenate(
                [
                    jnp.where(valid, gs_ref[j, pl.ds(c, times, stride=clips), :], 0.0).astype(BF16)
                    for j in group
                ],
                1,
            )
            lane = lax.broadcasted_iota(jnp.int32, (latents, wide), 1) // HD
            k = jnp.concatenate([kv_ref[pl.ds(s, lat), at : at + wide] for s in starts], 0)
            v = jnp.concatenate(
                [kv_ref[pl.ds(s, lat), width + at : width + at + wide] for s in starts], 0
            )
            zero = jnp.zeros_like(k)
            kx = jnp.concatenate([jnp.where(lane == h, k, zero) for h in range(heads)], 0)
            vx = jnp.concatenate([jnp.where(lane == h, v, zero) for h in range(heads)], 0)
            s = lax.dot_general(kx, q, NT, preferred_element_type=F32)
            gp = lax.dot_general(vx, g, NT, preferred_element_type=F32)
            s = s.reshape(heads, latents, times)
            gp = gp.reshape(heads, latents, times)
            e = jnp.exp(s - jnp.max(s, axis=1, keepdims=True))
            probs = e * (1.0 / jnp.sum(e, axis=1, keepdims=True))
            probs_low = probs.astype(BF16)
            row = jnp.sum(probs_low.astype(F32) * gp, axis=1, keepdims=True)
            grad = (probs * (gp - row)).astype(BF16).reshape(heads * latents, times)
            probs_low = probs_low.reshape(heads * latents, times)
            gq = lax.dot_general(grad, kx, TN, preferred_element_type=F32)
            for n, j in enumerate(group):
                qs[j, pl.ds(c, times, stride=clips), :] = gq[:, n * LANES : (n + 1) * LANES]
            gk = jnp.dot(grad, q, preferred_element_type=F32)
            gv = jnp.dot(probs_low, g, preferred_element_type=F32)

            def pick(full):
                out = full[:latents]
                for h in range(1, heads):
                    out = jnp.where(lane == h, full[h * latents : (h + 1) * latents], out)
                return out

            gk = (pick(gk) * scale).astype(BF16)
            gv = pick(gv).astype(BF16)
            for f in range(frames):
                part = slice(f * lat, (f + 1) * lat)
                gkv[pl.ds(starts[f], lat), at : at + wide] = gk[part]
                gkv[pl.ds(starts[f], lat), width + at : width + at + wide] = gv[part]
        return carry

    lax.fori_loop(0, clips, clip, 0, unroll=2)
    for at, size in spans(pool_ref.shape[1], 256):
        made = lax.dot_general(
            gkv[...], wkv[at : at + size, : 2 * width], NT, preferred_element_type=F32
        )
        pool_ref[:, at : at + size] = made.astype(BF16)
    for j in range(tiles):
        gq_ref[:, j * LANES : (j + 1) * LANES] = qs[j, 0:rows, :].astype(BF16)


def text_grad_kernel(text_ref, mean_ref, inv_ref, gain_ref, gq_ref, wq_ref, out_ref, acc):
    deep = wq_ref.shape[0]
    for at, size in spans(deep, 256):
        acc[:, at : at + size] = (
            lax.dot_general(
                gq_ref[...], wq_ref[at : at + size, :], NT, preferred_element_type=F32
            )
            * gain_ref[:, at : at + size]
        )
    rows = text_ref.shape[0]
    step = 88 if rows % 88 == 0 else rows
    for at, size in spans(rows, step):
        x = text_ref[at : at + size, :].astype(F32)
        inverse = inv_ref[at : at + size, 0:1]
        unit = (x - mean_ref[at : at + size, 0:1]) * inverse
        g = acc[at : at + size, :]
        first = jnp.mean(g, axis=1, keepdims=True)
        second = jnp.mean(g * unit, axis=1, keepdims=True)
        out_ref[at : at + size, :] = (inverse * (g - first - unit * second)).astype(BF16)


def shards(
    video_tokens,
    pool_weight,
    text_states,
    norm_gain,
    lengths,
    cotangent,
    query_weight,
    key_weight,
    value_weight,
    out_weight,
    *,
    count,
    frames,
):
    visual = video_tokens.shape[3]
    lat = pool_weight.shape[1]
    clips, times, model = text_states.shape
    width = query_weight.shape[1]
    depth = query_weight.shape[0]
    kv_rows = key_weight.shape[0]
    rows = clips * times
    full = clips * up(times, 16)
    latent_rows = frames * clips * lat
    out_rows = out_weight.shape[0]
    tall = up(out_rows, 8)
    wide = up(model, LANES)
    lanes = max(2 * width, wide)
    frame = lax.axis_index("frame")

    pack = jnp.concatenate(
        [
            jnp.pad(
                jnp.concatenate([key_weight, value_weight], 1),
                ((0, 0), (0, lanes - 2 * width)),
            ),
            jnp.pad(out_weight, ((0, tall - out_rows), (0, lanes - model))),
        ],
        0,
    )
    packs = pieces_of(pack, count)
    query_pieces = pieces_of(query_weight, count)

    pooled = jnp.einsum(
        "flp,cfpv->cflv", pool_weight, video_tokens, preferred_element_type=F32
    ).astype(BF16)
    pooled = pooled.reshape(frames, clips * lat, visual)
    blocks = []
    for shift in range(frames):
        block = lax.dynamic_index_in_dim(pooled, (frame + shift) % frames, 0, keepdims=False)
        if shift:
            block = lax.ppermute(block, "frame", [(i, (i + shift) % frames) for i in range(frames)])
        blocks.append(block)
    pool_rows = jnp.concatenate(blocks, 0)

    text = jnp.transpose(text_states, (1, 0, 2)).reshape(rows, model)
    cot = jnp.transpose(cotangent, (1, 0, 2)).reshape(rows, model)
    gain = norm_gain.reshape(1, model)

    normed, mean, inverse = pl.pallas_call(
        norm_kernel,
        name="norm",
        out_shape=(
            jax.ShapeDtypeStruct((rows, model), BF16),
            jax.ShapeDtypeStruct((rows, LANES), F32),
            jax.ShapeDtypeStruct((rows, LANES), F32),
        ),
        in_specs=[VMEM, VMEM],
        out_specs=(VMEM, VMEM, VMEM),
        compiler_params=params(),
        cost_estimate=cost(rows * model * 10, rows * model * 4),
    )(text, gain)

    keys_values, kv_full, grad_att = pl.pallas_call(
        functools.partial(project_kernel, count, out_rows),
        name="project",
        out_shape=(
            jax.ShapeDtypeStruct((latent_rows, 2 * width), BF16),
            jax.ShapeDtypeStruct((count * kv_rows, lanes), BF16),
            jax.ShapeDtypeStruct((width // LANES, full, LANES), F32),
        ),
        in_specs=[VMEM] * (count + 2),
        out_specs=(VMEM, VMEM, VMEM),
        scratch_shapes=[
            pltpu.VMEM((count, tall, wide), BF16),
            pltpu.VMEM((width, wide), BF16),
        ],
        compiler_params=params(),
        cost_estimate=cost(
            2 * rows * model * width + 4 * latent_rows * visual * width,
            4 * model * width + 4 * visual * width,
        ),
    )(*packs, pool_rows, cot)

    grad_queries, pool_grad, query_full = pl.pallas_call(
        functools.partial(attend_kernel, count, clips, frames),
        name="attend",
        out_shape=(
            jax.ShapeDtypeStruct((rows, width), BF16),
            jax.ShapeDtypeStruct((latent_rows, visual), BF16),
            jax.ShapeDtypeStruct((model, width), BF16),
        ),
        in_specs=[VMEM] * count + [SMEM, VMEM, VMEM, VMEM, VMEM],
        out_specs=(VMEM, VMEM, VMEM),
        scratch_shapes=[
            pltpu.VMEM((count, depth, width), BF16),
            pltpu.VMEM((width // LANES, full, LANES), F32),
            pltpu.VMEM((latent_rows, 2 * width), BF16),
        ],
        compiler_params=params(),
        cost_estimate=cost(4 * rows * model * width, 8 * model * width),
    )(*query_pieces, lengths, normed, grad_att, keys_values, kv_full)

    pool_grad = pool_grad.reshape(frames, clips, lat, visual)
    grad_pooled = jnp.zeros((frames, clips, lat, visual), BF16)
    for shift in range(frames):
        block = pool_grad[shift]
        if shift:
            block = lax.ppermute(
                block, "frame", [(i, (i - shift) % frames) for i in range(frames)]
            )
        grad_pooled = lax.dynamic_update_index_in_dim(
            grad_pooled, block, (frame + shift) % frames, 0
        )
    grad_pooled = grad_pooled.reshape(frames * clips, lat, visual)

    grad_text = pl.pallas_call(
        text_grad_kernel,
        name="text_grad",
        out_shape=jax.ShapeDtypeStruct((rows, model), BF16),
        in_specs=[VMEM] * 6,
        out_specs=VMEM,
        scratch_shapes=[pltpu.VMEM((rows, model), F32)],
        compiler_params=params(),
        cost_estimate=cost(2 * rows * model * width, 2 * model * width + 4 * rows * model),
    )(text, mean, inverse, gain, grad_queries, query_full)
    grad_text = jnp.transpose(grad_text.reshape(times, clips, model), (1, 0, 2))
    return (grad_text, grad_pooled)


def solution(mesh):
    in_specs = (
        P("dp", "frame", None, None),
        P("frame", None, None),
        P(("dp", "frame"), None, None),
        P(),
        P(("dp", "frame")),
        P(("dp", "frame"), None, None),
        P("dp", None),
        P("dp", None),
        P("dp", None),
        P("dp", None),
    )
    out_specs = (P(("dp", "frame"), None, None), P("dp", "frame", None))
    count = mesh.shape["dp"]
    body = functools.partial(shards, count=count, frames=mesh.shape["frame"])

    return jax.shard_map(body, mesh=mesh, in_specs=in_specs, out_specs=out_specs, check_vma=False)
```

```python
import functools

import jax
import jax.numpy as jnp
from jax import lax
from jax.experimental import pallas as pl
from jax.experimental.pallas import tpu as pltpu
from jax.sharding import PartitionSpec as P


HD = 64
EPSILON = 1e-05
F32 = jnp.float32
BF16 = jnp.bfloat16
LANES = 128
NT = (((1,), (1,)), ((), ()))
TN = (((0,), (0,)), ((), ()))
VMEM = pl.BlockSpec(memory_space=pltpu.VMEM)
SMEM = pl.BlockSpec(memory_space=pltpu.SMEM)


def up(value, unit):
    return -(-value // unit) * unit


def spans(total, step):
    return [(i, min(step, total - i)) for i in range(0, total, step)]


def params():
    return pltpu.CompilerParams(vmem_limit_bytes=32 * 1024 * 1024)


def cost(flops, nbytes):
    return pl.CostEstimate(flops=flops, bytes_accessed=nbytes, transcendentals=0)


def relayed(count):
    return count // 4 == 4


def pieces_of(own, count, tag):
    def move(array, pairs):
        return lax.ppermute(array, "dp", pairs)

    def along(pairs):
        return [(4 * a + i, 4 * b + i) for a, b in pairs for i in range(4)]

    def flip(mask):
        return [(i, i ^ mask) for i in range(count)]

    pieces = {0: own}
    parts = {}
    if relayed(count):
        place = lax.axis_index("dp") // 4
        inner = (place == 1) | (place == 2)
        swap, ends = along([(1, 2), (2, 1)]), along([(1, 0), (2, 3)])
        pieces[4] = move(own, flip(4))
        first = move(own, swap)
        second = move(pieces[4], swap)
        parts = {8: (first, move(first, ends)), 12: (second, move(second, ends))}
        for mask, (near, far) in parts.items():
            pieces[mask] = jnp.where(inner, near, far)
    else:
        for mask in range(4, count, 4):
            pieces[mask] = move(own, flip(mask))
    for mask in range(0, count, 4):
        if mask in parts and tag == "p":
            near, far = parts[mask]
            middle = [(i, j) for i, j in flip(2) if i // 4 in (1, 2)]
            outer = [(i, j) for i, j in flip(2) if i // 4 not in (1, 2)]
            near = move(near, middle)
            pieces[mask + 2] = jnp.where(inner, near, move(far, outer))
        elif mask + 2 < count:
            pieces[mask + 2] = move(pieces[mask], flip(2))
    for mask in range(0, count, 2):
        pieces[mask + 1] = move(pieces[mask], flip(1))
    return [pieces[mask] for mask in range(count)]


def sources(count):
    me = lax.axis_index("dp")
    inner = lax.rem(lax.div(lax.div(me, 4) + 1, 2), 2)
    turn = 4 * inner if relayed(count) else 0
    return [me ^ m ^ turn if m >= 8 else me ^ m for m in range(count)]


def project_kernel(count, out_rows, *refs):
    pieces = refs[:count]
    pool_ref, cot_ref, kv_ref, wkv, gs_ref, loose, wo = refs[count:]
    rows, model = cot_ref.shape
    tiles, full, _ = gs_ref.shape
    width = tiles * LANES
    depth = wkv.shape[0] // count
    _, tall, wide = loose.shape
    if full > rows:
        for j in range(tiles):
            gs_ref[j, rows:full, :] = jnp.zeros((full - rows, LANES), F32)
    for piece, source in zip(pieces, sources(count)):
        wkv[pl.ds(pl.multiple_of(source * depth, depth), depth), :] = piece[0:depth, :]
        loose[source] = piece[depth : depth + tall, 0:wide]
    for p in range(count):
        wo[p * out_rows : (p + 1) * out_rows, :] = loose[p, 0:out_rows, :]
    for at, size in spans(2 * width, 256):
        made = jnp.dot(pool_ref[...], wkv[:, at : at + size], preferred_element_type=F32)
        if at + size <= width:
            made = made.astype(BF16) * HD ** (-0.5)
        elif at < width:
            lane = at + lax.broadcasted_iota(jnp.int32, made.shape, 1)
            made = made * jnp.where(lane < width, HD ** (-0.5), 1.0)
        kv_ref[:, at : at + size] = made.astype(BF16)
    for at, size in spans(width, 256):
        made = lax.dot_general(
            cot_ref[...], wo[at : at + size, :model], NT, preferred_element_type=F32
        )
        made = made.astype(BF16).astype(F32)
        for part in range(0, size, LANES):
            gs_ref[(at + part) // LANES, 0:rows, :] = made[:, part : part + LANES]


def norm_kernel(text_ref, gain_ref, normed_ref, mean_ref, inv_ref):
    rows = text_ref.shape[0]
    step = 88 if rows % 88 == 0 else rows

    for at, size in spans(rows, step):
        x = text_ref[at : at + size, :].astype(F32)
        mean = jnp.mean(x, axis=1, keepdims=True)
        centered = x - mean
        inverse = lax.rsqrt(jnp.mean(centered * centered, axis=1, keepdims=True) + EPSILON)
        normed_ref[at : at + size, :] = (centered * inverse * gain_ref[...]).astype(BF16)
        mean_ref[at : at + size, :] = jnp.broadcast_to(mean, (size, LANES))
        inv_ref[at : at + size, :] = jnp.broadcast_to(inverse, (size, LANES))


def attend_kernel(count, clips, frames, *refs):
    pieces = refs[:count]
    lengths_ref, normed_ref, gs_ref, kv_ref, wkv, gq_ref, pool_ref, wq = refs[
        count : count + 8
    ]
    slots, qs, gkv = refs[count + 8 :]
    depth = pieces[0].shape[0]
    width = kv_ref.shape[1] // 2
    rows = normed_ref.shape[0]
    tiles, full, _ = qs.shape
    times = full // clips
    lat = kv_ref.shape[0] // (frames * clips)
    latents = lat * frames
    scale = HD ** (-0.5)
    for piece, source in zip(pieces, sources(count)):
        slots[source] = piece[...]
    if full > rows:
        for j in range(tiles):
            qs[j, rows:full, :] = jnp.zeros((full - rows, LANES), F32)
    for p in range(count):
        wq[p * depth : (p + 1) * depth, :] = slots[p]
    for at, size in spans(width, 256):
        made = jnp.dot(normed_ref[...], wq[:, at : at + size], preferred_element_type=F32)
        made = made.astype(BF16).astype(F32)
        for part in range(0, size, LANES):
            qs[(at + part) // LANES, 0:rows, :] = made[:, part : part + LANES]

    def clip(c, carry):
        length = lengths_ref[c]
        valid = lax.broadcasted_iota(jnp.int32, (times, LANES), 0) < length
        starts = [
            pl.multiple_of((f * clips + c) * lat, lat) for f in range(frames)
        ]
        for first in range(0, tiles, 2):
            group = range(first, min(first + 2, tiles))
            at = first * LANES
            wide = len(group) * LANES
            heads = wide // HD
            q = jnp.concatenate(
                [qs[j, pl.ds(c, times, stride=clips), :].astype(BF16) for j in group], 1
            )
            g = jnp.concatenate(
                [
                    jnp.where(valid, gs_ref[j, pl.ds(c, times, stride=clips), :], 0.0).astype(BF16)
                    for j in group
                ],
                1,
            )
            lane = lax.broadcasted_iota(jnp.int32, (latents, wide), 1) // HD
            k = jnp.concatenate([kv_ref[pl.ds(s, lat), at : at + wide] for s in starts], 0)
            v = jnp.concatenate(
                [kv_ref[pl.ds(s, lat), width + at : width + at + wide] for s in starts], 0
            )
            zero = jnp.zeros_like(k)
            kx = jnp.concatenate([jnp.where(lane == h, k, zero) for h in range(heads)], 0)
            vx = jnp.concatenate([jnp.where(lane == h, v, zero) for h in range(heads)], 0)
            s = lax.dot_general(kx, q, NT, preferred_element_type=F32)
            gp = lax.dot_general(vx, g, NT, preferred_element_type=F32)
            s = s.reshape(heads, latents, times)
            gp = gp.reshape(heads, latents, times)
            e = jnp.exp(s - jnp.max(s, axis=1, keepdims=True))
            probs = e * (1.0 / jnp.sum(e, axis=1, keepdims=True))
            probs_low = probs.astype(BF16)
            row = jnp.sum(probs_low.astype(F32) * gp, axis=1, keepdims=True)
            grad = (probs * (gp - row)).astype(BF16).reshape(heads * latents, times)
            probs_low = probs_low.reshape(heads * latents, times)
            gq = lax.dot_general(grad, kx, TN, preferred_element_type=F32)
            for n, j in enumerate(group):
                qs[j, pl.ds(c, times, stride=clips), :] = gq[:, n * LANES : (n + 1) * LANES]
            gk = jnp.dot(grad, q, preferred_element_type=F32)
            gv = jnp.dot(probs_low, g, preferred_element_type=F32)

            def pick(full):
                out = full[:latents]
                for h in range(1, heads):
                    out = jnp.where(lane == h, full[h * latents : (h + 1) * latents], out)
                return out

            gk = (pick(gk) * scale).astype(BF16)
            gv = pick(gv).astype(BF16)
            for f in range(frames):
                part = slice(f * lat, (f + 1) * lat)
                gkv[pl.ds(starts[f], lat), at : at + wide] = gk[part]
                gkv[pl.ds(starts[f], lat), width + at : width + at + wide] = gv[part]
        return carry

    lax.fori_loop(0, clips, clip, 0, unroll=2)
    for at, size in spans(pool_ref.shape[1], 256):
        made = lax.dot_general(
            gkv[...], wkv[at : at + size, : 2 * width], NT, preferred_element_type=F32
        )
        pool_ref[:, at : at + size] = made.astype(BF16)
    for j in range(tiles):
        gq_ref[:, j * LANES : (j + 1) * LANES] = qs[j, 0:rows, :].astype(BF16)


def text_grad_kernel(text_ref, mean_ref, inv_ref, gain_ref, gq_ref, wq_ref, out_ref, acc):
    deep = wq_ref.shape[0]
    for at, size in spans(deep, 256):
        acc[:, at : at + size] = (
            lax.dot_general(
                gq_ref[...], wq_ref[at : at + size, :], NT, preferred_element_type=F32
            )
            * gain_ref[:, at : at + size]
        )
    rows = text_ref.shape[0]
    step = 88 if rows % 88 == 0 else rows
    for at, size in spans(rows, step):
        x = text_ref[at : at + size, :].astype(F32)
        inverse = inv_ref[at : at + size, 0:1]
        unit = (x - mean_ref[at : at + size, 0:1]) * inverse
        g = acc[at : at + size, :]
        first = jnp.mean(g, axis=1, keepdims=True)
        second = jnp.mean(g * unit, axis=1, keepdims=True)
        out_ref[at : at + size, :] = (inverse * (g - first - unit * second)).astype(BF16)


def shards(
    video_tokens,
    pool_weight,
    text_states,
    norm_gain,
    lengths,
    cotangent,
    query_weight,
    key_weight,
    value_weight,
    out_weight,
    *,
    count,
    frames,
):
    visual = video_tokens.shape[3]
    lat = pool_weight.shape[1]
    clips, times, model = text_states.shape
    width = query_weight.shape[1]
    depth = query_weight.shape[0]
    kv_rows = key_weight.shape[0]
    rows = clips * times
    full = clips * up(times, 16)
    latent_rows = frames * clips * lat
    out_rows = out_weight.shape[0]
    tall = up(out_rows, 8)
    wide = up(model, LANES)
    lanes = max(2 * width, wide)
    frame = lax.axis_index("frame")

    pack = jnp.concatenate(
        [
            jnp.pad(
                jnp.concatenate([key_weight, value_weight], 1),
                ((0, 0), (0, lanes - 2 * width)),
            ),
            jnp.pad(out_weight, ((0, tall - out_rows), (0, lanes - model))),
        ],
        0,
    )
    packs = pieces_of(pack, count, "p")
    query_pieces = pieces_of(query_weight, count, "q")

    pooled = jnp.einsum(
        "flp,cfpv->cflv", pool_weight, video_tokens, preferred_element_type=F32
    ).astype(BF16)
    pooled = pooled.reshape(frames, clips * lat, visual)
    blocks = []
    for shift in range(frames):
        block = lax.dynamic_index_in_dim(pooled, (frame + shift) % frames, 0, keepdims=False)
        if shift:
            block = lax.ppermute(block, "frame", [(i, (i + shift) % frames) for i in range(frames)])
        blocks.append(block)
    pool_rows = jnp.concatenate(blocks, 0)

    text = jnp.transpose(text_states, (1, 0, 2)).reshape(rows, model)
    cot = jnp.transpose(cotangent, (1, 0, 2)).reshape(rows, model)
    gain = norm_gain.reshape(1, model)

    normed, mean, inverse = pl.pallas_call(
        norm_kernel,
        name="norm",
        out_shape=(
            jax.ShapeDtypeStruct((rows, model), BF16),
            jax.ShapeDtypeStruct((rows, LANES), F32),
            jax.ShapeDtypeStruct((rows, LANES), F32),
        ),
        in_specs=[VMEM, VMEM],
        out_specs=(VMEM, VMEM, VMEM),
        compiler_params=params(),
        cost_estimate=cost(rows * model * 10, rows * model * 4),
    )(text, gain)

    keys_values, kv_full, grad_att = pl.pallas_call(
        functools.partial(project_kernel, count, out_rows),
        name="project",
        out_shape=(
            jax.ShapeDtypeStruct((latent_rows, 2 * width), BF16),
            jax.ShapeDtypeStruct((count * kv_rows, lanes), BF16),
            jax.ShapeDtypeStruct((width // LANES, full, LANES), F32),
        ),
        in_specs=[VMEM] * (count + 2),
        out_specs=(VMEM, VMEM, VMEM),
        scratch_shapes=[
            pltpu.VMEM((count, tall, wide), BF16),
            pltpu.VMEM((width, wide), BF16),
        ],
        compiler_params=params(),
        cost_estimate=cost(
            2 * rows * model * width + 4 * latent_rows * visual * width,
            4 * model * width + 4 * visual * width,
        ),
    )(*packs, pool_rows, cot)

    grad_queries, pool_grad, query_full = pl.pallas_call(
        functools.partial(attend_kernel, count, clips, frames),
        name="attend",
        out_shape=(
            jax.ShapeDtypeStruct((rows, width), BF16),
            jax.ShapeDtypeStruct((latent_rows, visual), BF16),
            jax.ShapeDtypeStruct((model, width), BF16),
        ),
        in_specs=[VMEM] * count + [SMEM, VMEM, VMEM, VMEM, VMEM],
        out_specs=(VMEM, VMEM, VMEM),
        scratch_shapes=[
            pltpu.VMEM((count, depth, width), BF16),
            pltpu.VMEM((width // LANES, full, LANES), F32),
            pltpu.VMEM((latent_rows, 2 * width), BF16),
        ],
        compiler_params=params(),
        cost_estimate=cost(4 * rows * model * width, 8 * model * width),
    )(*query_pieces, lengths, normed, grad_att, keys_values, kv_full)

    pool_grad = pool_grad.reshape(frames, clips, lat, visual)
    grad_pooled = jnp.zeros((frames, clips, lat, visual), BF16)
    for shift in range(frames):
        block = pool_grad[shift]
        if shift:
            block = lax.ppermute(
                block, "frame", [(i, (i - shift) % frames) for i in range(frames)]
            )
        grad_pooled = lax.dynamic_update_index_in_dim(
            grad_pooled, block, (frame + shift) % frames, 0
        )
    grad_pooled = grad_pooled.reshape(frames * clips, lat, visual)

    grad_text = pl.pallas_call(
        text_grad_kernel,
        name="text_grad",
        out_shape=jax.ShapeDtypeStruct((rows, model), BF16),
        in_specs=[VMEM] * 6,
        out_specs=VMEM,
        scratch_shapes=[pltpu.VMEM((rows, model), F32)],
        compiler_params=params(),
        cost_estimate=cost(2 * rows * model * width, 2 * model * width + 4 * rows * model),
    )(text, mean, inverse, gain, grad_queries, query_full)
    grad_text = jnp.transpose(grad_text.reshape(times, clips, model), (1, 0, 2))
    return (grad_text, grad_pooled)


def solution(mesh):
    in_specs = (
        P("dp", "frame", None, None),
        P("frame", None, None),
        P(("dp", "frame"), None, None),
        P(),
        P(("dp", "frame")),
        P(("dp", "frame"), None, None),
        P("dp", None),
        P("dp", None),
        P("dp", None),
        P("dp", None),
    )
    out_specs = (P(("dp", "frame"), None, None), P("dp", "frame", None))
    count = mesh.shape["dp"]
    body = functools.partial(shards, count=count, frames=mesh.shape["frame"])

    return jax.shard_map(body, mesh=mesh, in_specs=in_specs, out_specs=out_specs, check_vma=False)
```
